512 devices in a mesh: pipe: 4 (over x), expert: 128 (over y, z, core).
Axes of the slice: x: 4, y: 8, z: 8, core: 2. Of those that a mesh axis runs over, the one named last changes fastest.
Arguments:
- out_grad: bfloat16 [4, 2, 8192, 7168], P('pipe', None, 'expert'), may hold values from -1.5 to 1.5
- expert_ids: int32 [4, 2, 8192, 8], P('pipe', None, 'expert'), may hold values from 0 to 383, as said below
- gate_values: float32 [4, 2, 8192, 8], P('pipe', None, 'expert'), may hold values from 0.05 to 1
- down_tiles: bfloat16 [4, 128, 512, 896], P('pipe', 'expert'), may hold values from -0.125 to 0.125
- hidden_saved: bfloat16 [4, 2, 512, 8192], P('pipe', None, None, 'expert'), may hold values from -0.59765625 to 0.59765625
Outputs:
- hidden_grad: bfloat16 [4, 2, 512, 8192], P('pipe', None, None, 'expert')
- down_grad: bfloat16 [4, 128, 512, 896], P('pipe', 'expert')
- gate_grad: float32 [4, 2, 8192, 8], P('pipe', None, 'expert')
The draws below stay inside these ranges and needn't reach their ends.
Inputs may be any that keep to these rules, and one draw needn't show every extreme that they name: `expert_ids`: each row names 8 different experts. The experts of the window are those below 4. Among the 64 rows of one device in one micro-batch of one section, no window expert is named by more than 4 rows, and in every micro-batch of every section one window expert is named by exactly 4 rows of every device.
All inputs are finite; a program needn't handle non-finite values.
Results may differ from the reference program's by a relative error of at most 0.0057.
Values may be sent and summed in bfloat16 or wider, within the bound.
A program may use at most 64 MiB of HBM per device.

```python
import math
import jax
import jax.numpy as jnp

D = 7168
FF = 2048
EXPERTS_ALL = 384
TOPK = 8
MICRO = 2
HSPLIT = 4
TOK_DEV = 64
CAP = 4
FSPLIT = 8
GROUP = 32
HID_DEV = 512
FCOLS = 896
EXP_WIN = 4
SLOTS = 512
TOKENS = 8192
N_PIPE = 4
N_EXPERT = 128


def draw_expert_ids(key, part):
    key_list = jax.random.split(key, 7)
    lead_shape = (N_PIPE, MICRO, N_EXPERT)
    hot_expert = jax.random.randint(key_list[0], (N_PIPE, MICRO, 1, 1), 0, EXP_WIN)
    full_device = jax.random.randint(key_list[6], (N_PIPE, MICRO, 1, 1), 0, N_EXPERT)
    cold_count = jax.random.randint(key_list[1], lead_shape + (EXP_WIN,), 0, CAP + 1)
    device_place = jnp.arange(N_EXPERT, dtype=jnp.int32)[None, None, :, None]
    expert_place = jnp.arange(EXP_WIN, dtype=jnp.int32)[None, None, None, :]
    counts = jnp.where((expert_place == hot_expert) | (device_place == full_device), CAP, cold_count)
    scores = jax.random.randint(key_list[2], lead_shape + (EXP_WIN, TOK_DEV), 0, 2 ** 20) * TOK_DEV + jnp.arange(TOK_DEV, dtype=jnp.int32)
    order_rank = jnp.argsort(jnp.argsort(scores, axis=-1, stable=True), axis=-1, stable=True)
    chosen = order_rank < counts[..., None]
    chosen = jnp.swapaxes(chosen, -1, -2)
    chosen = jnp.concatenate([chosen, jnp.zeros(lead_shape + (TOK_DEV, TOPK - EXP_WIN), jnp.bool_)], axis=-1)
    column = jnp.arange(TOPK, dtype=jnp.int32)
    group_count = EXPERTS_ALL // TOPK
    away_pick = jax.random.randint(key_list[3], lead_shape + (TOK_DEV, TOPK), 1, group_count)
    free_pick = jax.random.randint(key_list[4], lead_shape + (TOK_DEV, TOPK), 0, group_count)
    multiple = jnp.where(column < EXP_WIN, jnp.where(chosen, 0, away_pick), free_pick)
    listed = multiple * TOPK + column
    rotation = jax.random.randint(key_list[5], lead_shape + (TOK_DEV, 1), 0, TOPK)
    listed = jnp.take_along_axis(listed, (column - rotation) % TOPK, axis=-1)
    return listed.reshape(N_PIPE, MICRO, N_EXPERT * TOK_DEV, TOPK).astype(jnp.int32)


def shard_levels(key, shape, shards, smallest, high):
    def one(position, shards_of):
        draws = jax.random.uniform(jax.random.fold_in(jax.random.fold_in(key, 6), position), (shards_of,), jnp.float32, smallest / len(shards), high / len(shards))
        return jnp.repeat(jnp.exp(draws), shape[position] // shards_of).reshape((-1,) + (1,) * (len(shape) - position - 1))

    gain = one(*shards[0])
    for cut in shards[1:]:
        gain = gain * one(*cut)
    return gain


def normal_values(key, dims, deviation, limit, pieces=(), held_as=jnp.bfloat16):
    drawn = deviation * jax.random.normal(key, dims, jnp.float32)
    if pieces:
        drawn = drawn * shard_levels(key, dims, pieces, -0.22, 0.18)
    return jnp.clip(drawn, -limit, limit).astype(held_as)


def setup_inputs(seed: int = 0) -> dict:
    streams_of = jax.random.split(jax.random.key(seed), 6)
    return {
        "out_grad": normal_values(streams_of[0], (N_PIPE, MICRO, TOKENS, D), 0.25, 1.5, ((0, 4), (2, 128))),
        "expert_ids": draw_expert_ids(jax.random.fold_in(streams_of[5], 71), 0),
        "gate_values": jnp.clip(jnp.exp(math.log(1.0) - 2.9957323 * jax.random.uniform(streams_of[2], (N_PIPE, MICRO, TOKENS, TOPK), jnp.float32) ** shard_levels(streams_of[2], (N_PIPE, MICRO, TOKENS, TOPK), ((0, 4), (2, 128)), -0.2, 0.2)), 0.05, 1.0),
        "down_tiles": normal_values(streams_of[3], (N_PIPE, N_EXPERT, HID_DEV, FCOLS), FF ** -0.5, 0.125, ((0, 4), (1, 128))),
        "hidden_saved": normal_values(streams_of[4], (N_PIPE, MICRO, SLOTS, EXP_WIN * FF), 0.1, 0.59765625, ((0, 4), (3, 128))),
    }


def route_slots(routing):
    experts = jnp.arange(EXP_WIN, dtype=jnp.int32)
    named_mask = routing[:, :, None] == experts[None, None, :]
    hit_count = jnp.any(named_mask, axis=1).astype(jnp.int32)
    blocks = hit_count.reshape(N_EXPERT, TOK_DEV, EXP_WIN)
    slot_rank = jnp.cumsum(blocks, axis=1) - blocks
    block_base = (jnp.arange(N_EXPERT, dtype=jnp.int32) * CAP)[:, None, None]
    slot_index = (block_base + slot_rank).reshape(TOKENS, EXP_WIN).astype(jnp.int32)
    return named_mask, hit_count, slot_index


def tile_matrix(tiles):
    return tiles.reshape(HSPLIT, FSPLIT, HID_DEV, FCOLS).transpose(0, 2, 1, 3).reshape(FF, D)


def matrix_tiles(matrix):
    return matrix.reshape(HSPLIT, HID_DEV, FSPLIT, FCOLS).transpose(0, 2, 1, 3).reshape(GROUP, HID_DEV, FCOLS)


def reference(out_grad, expert_ids, gate_values, down_tiles, hidden_saved):
    group_size = GROUP
    hidden_grads = []
    down_grads = []
    gate_grads = []
    for section_index in range(N_PIPE):
        section_rows = out_grad[(section_index + 1) % N_PIPE]
        section_hidden = []
        section_gate = []
        totals = [jnp.zeros((FF, D), jnp.float32) for expert in range(EXP_WIN)]
        for micro_step in range(MICRO):
            token_rows = section_rows[micro_step]
            routing = expert_ids[section_index, micro_step]
            gate_rows = gate_values[section_index, micro_step]
            named_mask, hit_count, slot_index = route_slots(routing)
            gate_pick = jnp.sum(jnp.where(named_mask, gate_rows[:, :, None], jnp.float32(0.0)), axis=1)
            token_score = jnp.zeros((TOKENS, EXP_WIN), jnp.float32)
            grad_cols = []
            for expert in range(EXP_WIN):
                target = jnp.where(hit_count[:, expert] == 1, slot_index[:, expert], SLOTS).astype(jnp.int32)
                dispatched = jnp.zeros((SLOTS, D), jnp.bfloat16).at[target].set(token_rows, mode="drop")
                gate_slots = jnp.zeros((SLOTS,), jnp.bfloat16).at[target].set(gate_pick[:, expert].astype(jnp.bfloat16), mode="drop")
                gate_wide = gate_slots.astype(jnp.float32)
                weight = tile_matrix(down_tiles[section_index, expert * group_size:(expert + 1) * group_size])
                raw_grad = jnp.dot(dispatched, weight.T, preferred_element_type=jnp.float32)
                saved_rows = hidden_saved[section_index, micro_step, :, expert * FF:(expert + 1) * FF]
                grad_cols.append((gate_wide[:, None] * raw_grad).astype(jnp.bfloat16))
                slot_score = jnp.sum(saved_rows.astype(jnp.float32) * raw_grad, axis=1)
                picked = slot_score[jnp.minimum(slot_index[:, expert], SLOTS - 1)]
                token_score = token_score.at[:, expert].set(jnp.where(hit_count[:, expert] == 1, picked, jnp.float32(0.0)))
                scaled = (gate_wide[:, None] * saved_rows.astype(jnp.float32)).astype(jnp.bfloat16)
                totals[expert] = totals[expert] + jnp.dot(scaled.T, dispatched, preferred_element_type=jnp.float32)
            section_hidden.append(jnp.concatenate(grad_cols, axis=1))
            section_gate.append(jnp.sum(jnp.where(named_mask, token_score[:, None, :], jnp.float32(0.0)), axis=2))
        hidden_grads.append(jnp.stack(section_hidden))
        gate_grads.append(jnp.stack(section_gate))
        down_grads.append(jnp.concatenate([matrix_tiles(total.astype(jnp.bfloat16)) for total in totals], axis=0))
    return jnp.stack(hidden_grads), jnp.stack(down_grads), jnp.stack(gate_grads)
```

```python
import jax
import jax.numpy as jnp
from jax import lax
from jax.experimental import pallas as pl
from jax.experimental.pallas import tpu as pltpu
from jax.sharding import PartitionSpec as P

MICRO = 2
CAP = 4
UNIT = MICRO * CAP
ZSIDE = 8
ROW = 2 * ZSIDE
LINE = ZSIDE // 2
MESH = pl.DeviceIdType.MESH
F32 = jnp.float32
BF16 = jnp.bfloat16


def fetched(source, target, sem):
    return pltpu.make_async_copy(source, target, sem)


def arrived(block, sem):
    pltpu.make_async_copy(block, block, sem).wait()


def relay_kernel(
    sides,
    ids_ref,
    gates_ref,
    rows_hbm,
    weight_hbm,
    saved_ref,
    hidden_out,
    down_out,
    gate_out,
    rows,
    weight,
    pick_out,
    pick_in,
    row_out,
    row_in,
    disp,
    saved_all,
    scaled,
    part,
    part_in,
    peer_out,
    peer_in,
    gate_src,
    gate_row,
    gate_mid,
    gate_all,
    score_src,
    score_row,
    score_mid,
    score_all,
    load_sem,
    pick_sem,
    hop_send,
    hop_recv,
    row_send,
    row_recv,
    side_send,
    side_recv,
    saved_send,
    saved_recv,
    twin_sem,
    part_send,
    part_recv,
    peer_send,
    peer_recv,
    small_send,
    small_recv,
):
    pipes, yside = sides
    experts = yside // 2
    rounds = yside // 2
    tokens = ids_ref.shape[1]
    tok_dev = tokens // MICRO
    lanes = ROW * UNIT
    slots = saved_ref.shape[0] // MICRO
    hid = saved_ref.shape[1]
    fcols = weight.shape[1]
    pipe = lax.axis_index("pipe")
    place = lax.axis_index("expert")
    y = place // ROW
    zc = place % ROW
    z = zc // 2
    core = zc % 2
    z_line = z % LINE
    z_base = z - z_line
    before = lax.rem(pipe + pipes - 1, pipes)
    after = lax.rem(pipe + 1, pipes)
    expert = y // 2

    def remote(source, target, send, recv, where, section=pipe):
        return pltpu.make_async_remote_copy(
            src_ref=source,
            dst_ref=target,
            send_sem=send,
            recv_sem=recv,
            device_id=(section, where),
            device_id_type=MESH,
        )

    load_rows = fetched(rows_hbm, rows, load_sem.at[0])
    load_rows.start()
    load_weight = fetched(weight_hbm, weight, load_sem.at[1])
    load_weight.start()

    ids = ids_ref[...]
    gates = gates_ref[...]
    first = lax.broadcasted_iota(jnp.int32, (tokens, tokens), 0)
    second = lax.broadcasted_iota(jnp.int32, (tokens, tokens), 1)
    earlier = ((first < second) & (first // tok_dev == second // tok_dev)).astype(F32).astype(BF16)
    hits = []
    gate_tok = []
    for number in range(experts):
        named = ids == number
        hit = jnp.max(jnp.where(named, 1.0, 0.0), axis=0, keepdims=True)
        hits.append(jnp.broadcast_to(hit, (UNIT, tokens)))
        picked = jnp.sum(jnp.where(named, gates, 0.0), axis=0, keepdims=True)
        gate_tok.append(jnp.broadcast_to(picked, (UNIT, tokens)))
    hits = jnp.concatenate(hits, axis=0)
    gate_tok = jnp.concatenate(gate_tok, axis=0)
    rank = jnp.dot(hits.astype(BF16), earlier, preferred_element_type=F32)
    unit_row = lax.broadcasted_iota(jnp.int32, (experts * UNIT, tokens), 0) % UNIT
    token = lax.broadcasted_iota(jnp.int32, (experts * UNIT, tokens), 1)
    pick = jnp.where(
        (rank == (unit_row % CAP).astype(F32)) & (token // tok_dev == unit_row // CAP), hits, 0.0
    )
    pick_out[...] = pick.astype(BF16)
    send_pick = remote(pick_out, pick_in, pick_sem.at[0], pick_sem.at[1], place, after)
    send_pick.start()

    def row_cast(source, target, kind):
        own = fetched(source, target.at[zc], small_recv.at[kind])
        own.start()

        @pl.loop(1, ROW)
        def _(offset):
            peer = lax.rem(zc + offset, ROW)
            remote(
                source, target.at[zc], small_send.at[kind], small_recv.at[kind], y * ROW + peer
            ).start()

    def column_cast(source, target, kind):
        own = fetched(source, target.at[y], small_recv.at[kind])
        own.start()

        @pl.loop(1, yside)
        def _(offset):
            peer = lax.rem(y + offset, yside)
            remote(
                source, target.at[y], small_send.at[kind], small_recv.at[kind], peer * ROW + zc
            ).start()

    slot_row = lax.broadcasted_iota(jnp.int32, (experts * UNIT, lanes), 0) % UNIT
    slot_lane = lax.broadcasted_iota(jnp.int32, (experts * UNIT, lanes), 1)
    mine = slot_lane == zc * UNIT + slot_row
    gate_slot = jnp.sum(pick * gate_tok, axis=1, keepdims=True).astype(BF16).astype(F32)
    gate_lane = jnp.where(mine, gate_slot, 0.0)
    pieces = [
        jnp.sum(gate_lane[number * UNIT : (number + 1) * UNIT], axis=0, keepdims=True)
        for number in range(experts)
    ]
    pieces += [jnp.zeros((8 - experts, lanes), F32)]
    gate_src[...] = jnp.concatenate(pieces, axis=0)
    row_cast(gate_src, gate_row, 0)

    line_row = lax.broadcasted_iota(jnp.int32, (lanes, lanes), 0)
    line_col = lax.broadcasted_iota(jnp.int32, (lanes, lanes), 1)
    per_micro = ROW * CAP
    micro_of = line_row // per_micro
    within = line_row % per_micro
    order = (line_col == (within // CAP) * UNIT + micro_of * CAP + within % CAP).astype(F32).astype(BF16)
    for number in range(yside):
        block = jnp.concatenate(
            [
                saved_ref[micro * slots + number * per_micro : micro * slots + (number + 1) * per_micro, :]
                for micro in range(MICRO)
            ],
            axis=0,
        )
        turned = lax.dot_general(
            block, order, (((0,), (0,)), ((), ())), preferred_element_type=F32
        )
        saved_all[core, z_line, number] = turned.astype(BF16)
    for offset in range(1, LINE):
        target = z_base + lax.rem(z_line + offset, LINE)
        remote(
            saved_all.at[core, z_line],
            saved_all.at[core, z_line],
            saved_send.at[offset],
            saved_recv.at[offset],
            y * ROW + target * 2 + core,
        ).start()

    load_rows.wait()
    send_pick.wait_recv()
    chosen = pick_in[...]
    for block in range(2 * LINE):
        taken = jnp.dot(
            chosen, rows[:, block * fcols : (block + 1) * fcols], preferred_element_type=F32
        )
        for number in range(experts):
            row_out[number, block] = taken[number * UNIT : (number + 1) * UNIT].astype(BF16)
    hops = []
    for turn in range(rounds):
        even = (y + turn) % 2 == 0
        y_to = lax.rem(jnp.where(even, y + turn, y + yside - turn), yside)
        hop = remote(
            row_out.at[y_to // 2],
            row_in.at[turn],
            hop_send.at[turn],
            hop_recv.at[turn],
            y_to * ROW + zc,
            before,
        )
        hop.start()
        hops.append(hop)

    def source_of(y_at, turn):
        return lax.rem(jnp.where(y_at % 2 == 0, y_at + yside - turn, y_at + turn), yside)

    def spread(turn):
        hops[turn].wait_recv()
        slot = source_of(y, turn) * ROW + zc
        own = fetched(
            row_in.at[turn, z_line * 2 + core], disp.at[slot], row_recv.at[turn]
        )
        own.start()

        @pl.loop(1, ROW)
        def _(offset):
            peer = lax.rem(zc + offset, ROW)
            block = ((peer // 2) % LINE) * 2 + peer % 2
            remote(
                row_in.at[turn, block],
                disp.at[slot],
                row_send.at[turn],
                row_recv.at[turn],
                y * ROW + peer,
            ).start()

    partner = jnp.where(y % 2 == 0, y + 1, y - 1)
    twin = y * ROW + z * 2 + (1 - core)
    shares = []

    def receive(step, owned, turn):
        if owned:
            source = source_of(y, turn)
            region = disp.at[pl.ds(source * ROW, ROW)]
            arrived(region, row_recv.at[turn])
            remote(
                region, region, side_send.at[turn], side_recv.at[turn], partner * ROW + zc
            ).start()
        else:
            source = source_of(partner, turn)
            region = disp.at[pl.ds(source * ROW, ROW)]
            arrived(region, side_recv.at[turn])
        value = disp[pl.ds(source * ROW, ROW)].reshape(ROW * UNIT, fcols)
        product = lax.dot_general(
            weight[...], value, (((1,), (1,)), ((), ())), preferred_element_type=F32
        )
        part[step] = product.reshape(LINE, 2, hid, lanes)
        share = remote(
            part.at[step, :, 1 - core],
            part_in.at[step],
            part_send.at[step],
            part_recv.at[step],
            twin,
        )
        share.start()
        shares.append((source, share))

    def pass_on(step):
        shares[step][1].wait_recv()
        peer_out[step] = (part[step, :, core] + part_in[step]).astype(BF16)
        for offset in range(1, LINE):
            target = lax.rem(z_line + offset, LINE)
            remote(
                peer_out.at[step, target],
                peer_in.at[step, offset],
                peer_send.at[step, offset],
                peer_recv.at[step, offset],
                y * ROW + (z_base + target) * 2 + core,
            ).start()

    def finish(step):
        source = shares[step][0]
        for offset in range(1, LINE):
            arrived(peer_in.at[step, offset], peer_recv.at[step, offset])
        total = part[step, z_line, core] + part_in[step, z_line]
        for offset in range(1, LINE):
            total = total + peer_in[step, offset].astype(F32)
        kept = saved_all[core, z_line, source].astype(F32)
        score_src[pl.ds(source, 1), :] = jnp.sum(total * kept, axis=0, keepdims=True)
        gated = (gate_all[source, pl.ds(expert, 1), :] * total).astype(BF16)
        turned = lax.dot_general(
            order, gated, (((1,), (1,)), ((), ())), preferred_element_type=F32
        ).astype(BF16)
        for micro in range(MICRO):
            start = pl.multiple_of(micro * slots + source * per_micro, per_micro)
            hidden_out[pl.ds(start, per_micro), :] = turned[
                micro * per_micro : (micro + 1) * per_micro
            ]

    plan = []
    for turn in range(rounds):
        plan.append((True, turn))
        if turn >= 1:
            plan.append((False, turn - 1))
    plan.append((False, rounds - 1))

    spread(0)
    arrived(gate_row, small_recv.at[0])
    summed = gate_row[0]
    for number in range(1, ROW):
        summed = summed + gate_row[number]
    gate_mid[...] = summed
    column_cast(gate_mid, gate_all, 1)
    load_weight.wait()
    issued = 1
    for step, (owned, turn) in enumerate(plan):
        while issued < rounds and issued <= step + 1:
            spread(issued)
            issued += 1
        receive(step, owned, turn)
        if step >= 1:
            pass_on(step - 1)
        if step == 1:
            arrived(gate_all, small_recv.at[1])
        if step >= 2:
            finish(step - 2)
    last = len(plan) - 1
    pass_on(last)
    for offset in range(1, LINE):
        origin = lax.rem(z_line + LINE - offset, LINE)
        arrived(saved_all.at[core, origin], saved_recv.at[offset])
    share_saved = remote(
        saved_all.at[core], saved_all.at[core], twin_sem.at[0], twin_sem.at[1], twin
    )
    share_saved.start()
    if last >= 1:
        finish(last - 1)
    finish(last)
    row_cast(score_src, score_row, 2)
    arrived(saved_all.at[1 - core], twin_sem.at[1])
    for number in range(yside):
        scale = gate_all[number, pl.ds(expert, 1), :]
        for line in range(LINE):
            for side in range(2):
                at = (line * 2 + side) * hid
                scaled[at : at + hid, number * lanes : (number + 1) * lanes] = (
                    saved_all[side, line, number].astype(F32) * scale
                ).astype(BF16)
    arrived(score_row, small_recv.at[2])
    summed = score_row[0]
    for number in range(1, ROW):
        summed = summed + score_row[number]
    score_mid[...] = summed
    column_cast(score_mid, score_all, 3)
    width = 256
    for start in range(0, fcols, width):
        stop = min(start + width, fcols)
        value = disp[:, :, start:stop].reshape(yside * ROW * UNIT, stop - start)
        down_out[:, start:stop] = jnp.dot(
            scaled[...], value, preferred_element_type=F32
        ).astype(BF16)
    arrived(score_all, small_recv.at[3])
    lines = []
    for number in range(experts):
        both = score_all[2 * number, pl.ds(y, 1), :] + score_all[2 * number + 1, pl.ds(y, 1), :]
        lines.append(jnp.broadcast_to(both, (UNIT, lanes)))
    slot_score = jnp.sum(
        jnp.where(mine, jnp.concatenate(lines, axis=0), 0.0), axis=1, keepdims=True
    )
    spread_score = pick * slot_score
    result = jnp.zeros(ids.shape, F32)
    for number in range(experts):
        by_token = jnp.sum(
            spread_score[number * UNIT : (number + 1) * UNIT], axis=0, keepdims=True
        )
        result = result + jnp.where(ids == number, by_token, 0.0)
    gate_out[...] = result

    send_pick.wait_send()
    for turn in range(rounds):
        hops[turn].wait_send()
        arrived(disp.at[pl.ds(0, ROW - 1)], row_send.at[turn])
        arrived(disp.at[pl.ds(0, ROW)], side_send.at[turn])
    for offset in range(1, LINE):
        arrived(saved_all.at[0, 0], saved_send.at[offset])
    share_saved.wait_send()
    for step in range(len(plan)):
        shares[step][1].wait_send()
        for offset in range(1, LINE):
            arrived(peer_out.at[step, 0], peer_send.at[step, offset])
    for kind, count, block in (
        (0, ROW - 1, gate_row),
        (1, yside - 1, gate_all),
        (2, ROW - 1, score_row),
        (3, yside - 1, score_all),
    ):
        arrived(block.at[pl.ds(0, count)], small_send.at[kind])


def body(out_grad, expert_ids, gate_values, down_tiles, hidden_saved):
    pipes = lax.axis_size("pipe")
    devices = lax.axis_size("expert")
    yside = devices // ROW
    rounds = yside // 2
    steps = yside
    experts = yside // 2
    _, micro, tok_dev, width = out_grad.shape
    _, _, tile_rows, tile_cols = down_tiles.shape
    _, _, slots, hid = hidden_saved.shape
    topk = expert_ids.shape[-1]
    tokens = micro * tok_dev
    lanes = ROW * UNIT
    ids = expert_ids.reshape(tokens, topk).T
    gates = gate_values.reshape(tokens, topk).T
    vmem = pl.BlockSpec(memory_space=pltpu.VMEM)
    anywhere = pl.BlockSpec(memory_space=pl.ANY)
    dma = pltpu.SemaphoreType.DMA
    hidden_grad, down_grad, gate_grad = pl.pallas_call(
        lambda *refs: relay_kernel((pipes, yside), *refs),
        out_shape=(
            jax.ShapeDtypeStruct((micro * slots, hid), BF16),
            jax.ShapeDtypeStruct((tile_rows, tile_cols), BF16),
            jax.ShapeDtypeStruct((topk, tokens), F32),
        ),
        in_specs=[vmem, vmem, anywhere, anywhere, vmem],
        out_specs=(vmem, vmem, vmem),
        scratch_shapes=[
            pltpu.VMEM((tokens, width), BF16),
            pltpu.VMEM((tile_rows, tile_cols), BF16),
            pltpu.VMEM((experts * UNIT, tokens), BF16),
            pltpu.VMEM((experts * UNIT, tokens), BF16),
            pltpu.VMEM((experts, 2 * LINE, UNIT, tile_cols), BF16),
            pltpu.VMEM((rounds, 2 * LINE, UNIT, tile_cols), BF16),
            pltpu.VMEM((devices, UNIT, tile_cols), BF16),
            pltpu.VMEM((2, LINE, yside, hid, lanes), BF16),
            pltpu.VMEM((tile_rows, yside * lanes), BF16),
            pltpu.VMEM((steps, LINE, 2, hid, lanes), F32),
            pltpu.VMEM((steps, LINE, hid, lanes), F32),
            pltpu.VMEM((steps, LINE, hid, lanes), BF16),
            pltpu.VMEM((steps, LINE, hid, lanes), BF16),
            pltpu.VMEM((8, lanes), F32),
            pltpu.VMEM((ROW, 8, lanes), F32),
            pltpu.VMEM((8, lanes), F32),
            pltpu.VMEM((yside, 8, lanes), F32),
            pltpu.VMEM((yside, lanes), F32),
            pltpu.VMEM((ROW, yside, lanes), F32),
            pltpu.VMEM((yside, lanes), F32),
            pltpu.VMEM((yside, yside, lanes), F32),
            dma((2,)),
            dma((2,)),
            dma((rounds,)),
            dma((rounds,)),
            dma((rounds,)),
            dma((rounds,)),
            dma((rounds,)),
            dma((rounds,)),
            dma((LINE,)),
            dma((LINE,)),
            dma((2,)),
            dma((steps,)),
            dma((steps,)),
            dma((steps, LINE)),
            dma((steps, LINE)),
            dma((4,)),
            dma((4,)),
        ],
        compiler_params=pltpu.CompilerParams(
            has_side_effects=True, vmem_limit_bytes=40 * 2**20
        ),
        name="relay",
    )(
        ids,
        gates,
        out_grad.reshape(tokens, width),
        down_tiles.reshape(tile_rows, tile_cols),
        hidden_saved.reshape(micro * slots, hid),
    )
    return (
        hidden_grad.reshape(1, micro, slots, hid),
        down_grad.reshape(1, 1, tile_rows, tile_cols),
        gate_grad.T.reshape(1, micro, tok_dev, topk),
    )


def solution(mesh):
    return jax.shard_map(
        body,
        mesh=mesh,
        in_specs=(
            P("pipe", None, "expert", None),
            P("pipe", None, "expert", None),
            P("pipe", None, "expert", None),
            P("pipe", "expert", None, None),
            P("pipe", None, None, "expert"),
        ),
        out_specs=(
            P("pipe", None, None, "expert"),
            P("pipe", "expert", None, None),
            P("pipe", None, "expert", None),
        ),
        check_vma=False,
    )
```

```python
import jax
import jax.numpy as jnp
from jax import lax
from jax.experimental import pallas as pl
from jax.experimental.pallas import tpu as pltpu
from jax.sharding import PartitionSpec as P

MICRO = 2
CAP = 4
UNIT = MICRO * CAP
ZSIDE = 8
ROW = 2 * ZSIDE
LINE = ZSIDE // 2
MESH = pl.DeviceIdType.MESH
F32 = jnp.float32
BF16 = jnp.bfloat16


def fetched(source, target, sem):
    return pltpu.make_async_copy(source, target, sem)


def arrived(block, sem):
    pltpu.make_async_copy(block, block, sem).wait()


def relay_kernel(
    sides,
    ids_ref,
    gates_ref,
    rows_hbm,
    weight_hbm,
    saved_hbm,
    hidden_out,
    down_out,
    gate_out,
    rows,
    weight,
    saved,
    pick_out,
    pick_in,
    row_out,
    row_in,
    disp,
    saved_all,
    total,
    part,
    part_in,
    peer_out,
    peer_in,
    gate_src,
    gate_row,
    gate_mid,
    gate_all,
    score_src,
    score_col,
    score_mid,
    score_row,
    turned_all,
    load_sem,
    pick_sem,
    hop_send,
    hop_recv,
    row_send,
    row_recv,
    side_send,
    side_recv,
    saved_send,
    saved_recv,
    twin_sem,
    part_send,
    part_recv,
    peer_send,
    peer_recv,
    small_send,
    small_recv,
):
    pipes, yside = sides
    experts = yside // 2
    rounds = yside // 2
    tok_dev = ids_ref.shape[2]
    tokens = tok_dev * MICRO
    lanes = ROW * UNIT
    hid = saved.shape[1]
    fcols = weight.shape[1]
    pipe = lax.axis_index("pipe")
    place = lax.axis_index("expert")
    y = place // ROW
    zc = place % ROW
    z = zc // 2
    core = zc % 2
    z_line = z % LINE
    z_base = z - z_line
    before = lax.rem(pipe + pipes - 1, pipes)
    after = lax.rem(pipe + 1, pipes)
    expert = y // 2

    def remote(source, target, send, recv, where, section=pipe):
        return pltpu.make_async_remote_copy(
            src_ref=source,
            dst_ref=target,
            send_sem=send,
            recv_sem=recv,
            device_id=(section, where),
            device_id_type=MESH,
        )

    def source_of(y_at, turn):
        return lax.rem(jnp.where(y_at % 2 == 0, y_at + yside - turn, y_at + turn), yside)

    barrier = pltpu.get_barrier_semaphore()

    def greet(where, section=pipe):
        pl.semaphore_signal(barrier, inc=1, device_id=(section, where), device_id_type=MESH)

    greet(place, before)
    for turn in range(rounds):
        greet(source_of(y, turn) * ROW + zc, after)
    for offset in range(1, ROW):
        greet(y * ROW + lax.rem(zc + offset, ROW))
    for offset in range(1, yside):
        greet(lax.rem(y + offset, yside) * ROW + zc)

    load_rows = fetched(rows_hbm, rows, load_sem.at[0])
    load_rows.start()
    load_saved = fetched(saved_hbm, saved, load_sem.at[2])
    load_saved.start()
    load_weight = fetched(weight_hbm, weight, load_sem.at[1])
    load_weight.start()

    ids = jnp.concatenate([ids_ref[micro] for micro in range(MICRO)], axis=1)
    gates = jnp.concatenate([gates_ref[micro] for micro in range(MICRO)], axis=1)
    first = lax.broadcasted_iota(jnp.int32, (tokens, tokens), 0)
    second = lax.broadcasted_iota(jnp.int32, (tokens, tokens), 1)
    earlier = ((first < second) & (first // tok_dev == second // tok_dev)).astype(F32).astype(BF16)
    hits = []
    gate_tok = []
    for number in range(experts):
        named = ids == number
        hit = jnp.max(jnp.where(named, 1.0, 0.0), axis=0, keepdims=True)
        hits.append(jnp.broadcast_to(hit, (UNIT, tokens)))
        picked = jnp.sum(jnp.where(named, gates, 0.0), axis=0, keepdims=True)
        gate_tok.append(jnp.broadcast_to(picked, (UNIT, tokens)))
    hits = jnp.concatenate(hits, axis=0)
    gate_tok = jnp.concatenate(gate_tok, axis=0)
    rank = jnp.dot(hits.astype(BF16), earlier, preferred_element_type=F32)
    unit_row = lax.broadcasted_iota(jnp.int32, (experts * UNIT, tokens), 0) % UNIT
    token = lax.broadcasted_iota(jnp.int32, (experts * UNIT, tokens), 1)
    pick = jnp.where(
        (rank == (unit_row % CAP).astype(F32)) & (token // tok_dev == unit_row // CAP), hits, 0.0
    )
    pick_out[...] = pick.astype(BF16)
    pl.semaphore_wait(barrier, 1 + rounds + ROW - 1 + yside - 1)
    send_pick = remote(pick_out, pick_in, pick_sem.at[0], pick_sem.at[1], place, after)
    send_pick.start()

    def row_cast(source, target, kind):
        own = fetched(source, target.at[zc], small_recv.at[kind])
        own.start()

        @pl.loop(1, ROW)
        def _(offset):
            peer = lax.rem(zc + offset, ROW)
            remote(
                source, target.at[zc], small_send.at[kind], small_recv.at[kind], y * ROW + peer
            ).start()

    def column_cast(source, target, kind):
        own = fetched(source, target.at[y], small_recv.at[kind])
        own.start()

        @pl.loop(1, yside)
        def _(offset):
            peer = lax.rem(y + offset, yside)
            remote(
                source, target.at[y], small_send.at[kind], small_recv.at[kind], peer * ROW + zc
            ).start()

    slot_row = lax.broadcasted_iota(jnp.int32, (experts * UNIT, lanes), 0) % UNIT
    slot_lane = lax.broadcasted_iota(jnp.int32, (experts * UNIT, lanes), 1)
    mine = slot_lane == zc * UNIT + slot_row
    gate_slot = jnp.sum(pick * gate_tok, axis=1, keepdims=True).astype(BF16).astype(F32)
    gate_lane = jnp.where(mine, gate_slot, 0.0)
    pieces = [
        jnp.sum(gate_lane[number * UNIT : (number + 1) * UNIT], axis=0, keepdims=True)
        for number in range(experts)
    ]
    pieces += [jnp.zeros((8 - experts, lanes), F32)]
    gate_src[...] = jnp.concatenate(pieces, axis=0)
    row_cast(gate_src, gate_row, 0)

    line_row = lax.broadcasted_iota(jnp.int32, (lanes, lanes), 0)
    line_col = lax.broadcasted_iota(jnp.int32, (lanes, lanes), 1)
    per_micro = ROW * CAP
    micro_of = line_row // per_micro
    within = line_row % per_micro
    order = (line_col == (within // CAP) * UNIT + micro_of * CAP + within % CAP).astype(F32).astype(BF16)
    load_saved.wait()
    for number in range(yside):
        block = jnp.concatenate(
            [
                saved[micro, :, number * per_micro : (number + 1) * per_micro]
                for micro in range(MICRO)
            ],
            axis=1,
        )
        saved_all[core, z_line, number] = jnp.dot(
            block, order, preferred_element_type=F32
        ).astype(BF16)
    for offset in range(1, LINE):
        target = z_base + lax.rem(z_line + offset, LINE)
        remote(
            saved_all.at[core, z_line],
            saved_all.at[core, z_line],
            saved_send.at[offset],
            saved_recv.at[offset],
            y * ROW + target * 2 + core,
        ).start()

    load_rows.wait()
    send_pick.wait_recv()
    chosen = pick_in[...]
    for block in range(2 * LINE):
        taken = jnp.dot(
            chosen, rows[:, block * fcols : (block + 1) * fcols], preferred_element_type=F32
        )
        for number in range(experts):
            row_out[number, block] = taken[number * UNIT : (number + 1) * UNIT].astype(BF16)
    hops = []
    for turn in range(rounds):
        even = (y + turn) % 2 == 0
        y_to = lax.rem(jnp.where(even, y + turn, y + yside - turn), yside)
        hop = remote(
            row_out.at[y_to // 2],
            row_in.at[turn],
            hop_send.at[turn],
            hop_recv.at[turn],
            y_to * ROW + zc,
            before,
        )
        hop.start()
        hops.append(hop)

    def spread(turn):
        hops[turn].wait_recv()
        slot = source_of(y, turn) * ROW + zc
        own = fetched(
            row_in.at[turn, z_line * 2 + core], disp.at[slot], row_recv.at[turn]
        )
        own.start()

        @pl.loop(1, ROW)
        def _(offset):
            peer = lax.rem(zc + offset, ROW)
            block = ((peer // 2) % LINE) * 2 + peer % 2
            remote(
                row_in.at[turn, block],
                disp.at[slot],
                row_send.at[turn],
                row_recv.at[turn],
                y * ROW + peer,
            ).start()

    partner = jnp.where(y % 2 == 0, y + 1, y - 1)
    twin = y * ROW + z * 2 + (1 - core)
    shares = []

    def receive(step, owned, turn):
        if owned:
            source = source_of(y, turn)
            region = disp.at[pl.ds(source * ROW, ROW)]
            arrived(region, row_recv.at[turn])
            remote(
                region, region, side_send.at[turn], side_recv.at[turn], partner * ROW + zc
            ).start()
        else:
            source = source_of(partner, turn)
            region = disp.at[pl.ds(source * ROW, ROW)]
            arrived(region, side_recv.at[turn])
        value = disp[pl.ds(source * ROW, ROW)].reshape(ROW * UNIT, fcols)
        product = lax.dot_general(
            weight[...], value, (((1,), (1,)), ((), ())), preferred_element_type=F32
        )
        part[step] = product.reshape(LINE, 2, hid, lanes)
        share = remote(
            part.at[step, :, 1 - core],
            part_in.at[step],
            part_send.at[step],
            part_recv.at[step],
            twin,
        )
        share.start()
        shares.append((source, share))
        if step == 0:
            arrived(saved_all.at[1 - core], twin_sem.at[1])
        score = jnp.zeros((hid, lanes), F32)
        for line in range(LINE):
            for side in range(2):
                at = (line * 2 + side) * hid
                score += saved_all[side, line, source].astype(F32) * product[at : at + hid]
        score_src[step] = jnp.sum(score, axis=0, keepdims=True)
        if owned and turn == 0:
            fetched(score_src.at[step], score_col.at[y], small_recv.at[2]).start()
        else:
            remote(
                score_src.at[step],
                score_col.at[y],
                small_send.at[2],
                small_recv.at[2],
                source * ROW + zc,
            ).start()

    def pass_on(step):
        shares[step][1].wait_recv()
        peer_out[step] = (part[step, :, core] + part_in[step]).astype(BF16)
        for offset in range(1, LINE):
            target = lax.rem(z_line + offset, LINE)
            remote(
                peer_out.at[step, target],
                peer_in.at[step, offset],
                peer_send.at[step, offset],
                peer_recv.at[step, offset],
                y * ROW + (z_base + target) * 2 + core,
            ).start()

    def finish(step):
        source = shares[step][0]
        for offset in range(1, LINE):
            arrived(peer_in.at[step, offset], peer_recv.at[step, offset])
        whole = part[step, z_line, core] + part_in[step, z_line]
        for offset in range(1, LINE):
            whole = whole + peer_in[step, offset].astype(F32)
        gated = (gate_all[source, pl.ds(expert, 1), :] * whole).astype(BF16)
        turned_all[source] = lax.dot_general(
            gated, order, (((1,), (1,)), ((), ())), preferred_element_type=F32
        ).astype(BF16)

    def grow(step):
        source = shares[step][0]
        scale = gate_all[source, pl.ds(expert, 1), :]
        left = jnp.concatenate(
            [
                (saved_all[side, line, source].astype(F32) * scale).astype(BF16)
                for line in range(LINE)
                for side in range(2)
            ],
            axis=0,
        )
        value = disp[pl.ds(source * ROW, ROW)].reshape(ROW * UNIT, fcols)
        update = jnp.dot(left, value, preferred_element_type=F32)
        if step > 0:
            update = total[...] + update
        if step < yside - 1:
            total[...] = update
        else:
            down_out[...] = update.astype(BF16)

    plan = []
    for turn in range(rounds):
        plan.append((True, turn))
        if turn >= 1:
            plan.append((False, turn - 1))
    plan.append((False, rounds - 1))

    for turn in range(rounds):
        spread(turn)
        if turn == 0:
            arrived(gate_row, small_recv.at[0])
            summed = gate_row[0]
            for number in range(1, ROW):
                summed = summed + gate_row[number]
            gate_mid[...] = summed
            column_cast(gate_mid, gate_all, 1)
            for offset in range(1, LINE):
                origin = lax.rem(z_line + LINE - offset, LINE)
                arrived(saved_all.at[core, origin], saved_recv.at[offset])
            share_saved = remote(
                saved_all.at[core], saved_all.at[core], twin_sem.at[0], twin_sem.at[1], twin
            )
            share_saved.start()
    load_weight.wait()
    for step, (owned, turn) in enumerate(plan):
        receive(step, owned, turn)
        if step == 0:
            arrived(gate_all, small_recv.at[1])
        if step >= 1:
            pass_on(step - 1)
        grow(step)
        if step >= 2:
            finish(step - 2)
    last = len(plan) - 1
    pass_on(last)
    arrived(score_col, small_recv.at[2])
    lines = [score_col[2 * number] + score_col[2 * number + 1] for number in range(experts)]
    lines += [jnp.zeros((8 - experts, lanes), F32)]
    score_mid[...] = jnp.concatenate(lines, axis=0)
    row_cast(score_mid, score_row, 3)
    if last >= 1:
        finish(last - 1)
    finish(last)
    for micro in range(MICRO):
        hidden_out[micro] = jnp.concatenate(
            [
                turned_all[number, :, micro * per_micro : (micro + 1) * per_micro]
                for number in range(yside)
            ],
            axis=1,
        )
    arrived(score_row, small_recv.at[3])
    summed = score_row[0]
    for number in range(1, ROW):
        summed = summed + score_row[number]
    lines = [
        jnp.broadcast_to(summed[number : number + 1], (UNIT, lanes)) for number in range(experts)
    ]
    slot_score = jnp.sum(
        jnp.where(mine, jnp.concatenate(lines, axis=0), 0.0), axis=1, keepdims=True
    )
    spread_score = pick * slot_score
    result = jnp.zeros(ids.shape, F32)
    for number in range(experts):
        by_token = jnp.sum(
            spread_score[number * UNIT : (number + 1) * UNIT], axis=0, keepdims=True
        )
        result = result + jnp.where(ids == number, by_token, 0.0)
    for micro in range(MICRO):
        gate_out[micro] = result[:, micro * tok_dev : (micro + 1) * tok_dev]

    send_pick.wait_send()
    for turn in range(rounds):
        hops[turn].wait_send()
        arrived(disp.at[pl.ds(0, ROW - 1)], row_send.at[turn])
        arrived(disp.at[pl.ds(0, ROW)], side_send.at[turn])
    for offset in range(1, LINE):
        arrived(saved_all.at[0, 0], saved_send.at[offset])
    share_saved.wait_send()
    for step in range(len(plan)):
        shares[step][1].wait_send()
        for offset in range(1, LINE):
            arrived(peer_out.at[step, 0], peer_send.at[step, offset])
    for kind, count, block in (
        (0, ROW - 1, gate_row),
        (1, yside - 1, gate_all),
        (2, yside - 1, score_col),
        (3, ROW - 1, score_row),
    ):
        arrived(block.at[pl.ds(0, count)], small_send.at[kind])


def body(out_grad, expert_ids, gate_values, down_tiles, hidden_saved):
    pipes = lax.axis_size("pipe")
    devices = lax.axis_size("expert")
    yside = devices // ROW
    rounds = yside // 2
    steps = yside
    experts = yside // 2
    _, micro, tok_dev, width = out_grad.shape
    _, _, tile_rows, tile_cols = down_tiles.shape
    _, _, slots, hid = hidden_saved.shape
    topk = expert_ids.shape[-1]
    tokens = micro * tok_dev
    lanes = ROW * UNIT
    ids = expert_ids.transpose(0, 1, 3, 2).reshape(micro, topk, tok_dev)
    gates = gate_values.transpose(0, 1, 3, 2).reshape(micro, topk, tok_dev)
    saved = hidden_saved.transpose(0, 1, 3, 2).reshape(micro, hid, slots)
    vmem = pl.BlockSpec(memory_space=pltpu.VMEM)
    far = pl.BlockSpec(memory_space=pltpu.HBM)
    dma = pltpu.SemaphoreType.DMA
    hidden_grad, down_grad, gate_grad = pl.pallas_call(
        lambda *refs: relay_kernel((pipes, yside), *refs),
        out_shape=(
            jax.ShapeDtypeStruct((micro, hid, slots), BF16),
            jax.ShapeDtypeStruct((tile_rows, tile_cols), BF16),
            jax.ShapeDtypeStruct((micro, topk, tok_dev), F32),
        ),
        in_specs=[vmem, vmem, far, far, far],
        out_specs=(vmem, vmem, vmem),
        scratch_shapes=[
            pltpu.VMEM((tokens, width), BF16),
            pltpu.VMEM((tile_rows, tile_cols), BF16),
            pltpu.VMEM((micro, hid, slots), BF16),
            pltpu.VMEM((experts * UNIT, tokens), BF16),
            pltpu.VMEM((experts * UNIT, tokens), BF16),
            pltpu.VMEM((experts, 2 * LINE, UNIT, tile_cols), BF16),
            pltpu.VMEM((rounds, 2 * LINE, UNIT, tile_cols), BF16),
            pltpu.VMEM((devices, UNIT, tile_cols), BF16),
            pltpu.VMEM((2, LINE, yside, hid, lanes), BF16),
            pltpu.VMEM((tile_rows, tile_cols), F32),
            pltpu.VMEM((steps, LINE, 2, hid, lanes), F32),
            pltpu.VMEM((steps, LINE, hid, lanes), F32),
            pltpu.VMEM((steps, LINE, hid, lanes), BF16),
            pltpu.VMEM((steps, LINE, hid, lanes), BF16),
            pltpu.VMEM((8, lanes), F32),
            pltpu.VMEM((ROW, 8, lanes), F32),
            pltpu.VMEM((8, lanes), F32),
            pltpu.VMEM((yside, 8, lanes), F32),
            pltpu.VMEM((yside, 1, lanes), F32),
            pltpu.VMEM((yside, 1, lanes), F32),
            pltpu.VMEM((8, lanes), F32),
            pltpu.VMEM((ROW, 8, lanes), F32),
            pltpu.VMEM((yside, hid, lanes), BF16),
            dma((3,)),
            dma((2,)),
            dma((rounds,)),
            dma((rounds,)),
            dma((rounds,)),
            dma((rounds,)),
            dma((rounds,)),
            dma((rounds,)),
            dma((LINE,)),
            dma((LINE,)),
            dma((2,)),
            dma((steps,)),
            dma((steps,)),
            dma((steps, LINE)),
            dma((steps, LINE)),
            dma((4,)),
            dma((4,)),
        ],
        compiler_params=pltpu.CompilerParams(
            has_side_effects=True, collective_id=0, vmem_limit_bytes=62 * 2**20
        ),
        name="relay",
    )(
        ids,
        gates,
        out_grad.reshape(tokens, width),
        down_tiles.reshape(tile_rows, tile_cols),
        saved,
    )
    return (
        hidden_grad.reshape(1, micro, hid, slots).transpose(0, 1, 3, 2),
        down_grad.reshape(1, 1, tile_rows, tile_cols),
        gate_grad.reshape(1, micro, topk, tok_dev).transpose(0, 1, 3, 2),
    )


def solution(mesh):
    return jax.shard_map(
        body,
        mesh=mesh,
        in_specs=(
            P("pipe", None, "expert", None),
            P("pipe", None, "expert", None),
            P("pipe", None, "expert", None),
            P("pipe", "expert", None, None),
            P("pipe", None, None, "expert"),
        ),
        out_specs=(
            P("pipe", None, None, "expert"),
            P("pipe", "expert", None, None),
            P("pipe", None, "expert", None),
        ),
        check_vma=False,
    )
```

```python
import jax
import jax.numpy as jnp
from jax import lax
from jax.experimental import pallas as pl
from jax.experimental.pallas import tpu as pltpu
from jax.sharding import PartitionSpec as P

MICRO = 2
CAP = 4
UNIT = MICRO * CAP
ZSIDE = 8
ROW = 2 * ZSIDE
LINE = ZSIDE // 2
DEPTH = 2
DIRECT = 2
MESH = pl.DeviceIdType.MESH
F32 = jnp.float32
BF16 = jnp.bfloat16


def fetched(source, target, sem):
    return pltpu.make_async_copy(source, target, sem)


def arrived(block, sem):
    pltpu.make_async_copy(block, block, sem).wait()


def relay_kernel(
    sides,
    ids_ref,
    gates_ref,
    rows_hbm,
    weight_hbm,
    saved_hbm,
    hidden_out,
    down_out,
    gate_out,
    rows,
    weight,
    saved,
    pick_out,
    pick_in,
    row_out,
    row_in,
    disp,
    saved_all,
    total,
    part,
    part_in,
    peer_out,
    peer_in,
    fold_out,
    gate_src,
    gate_row,
    gate_mid,
    gate_all,
    score_src,
    score_col,
    score_mid,
    score_row,
    turned_all,
    load_sem,
    pick_sem,
    hop_send,
    hop_recv,
    row_send,
    row_recv,
    side_send,
    side_recv,
    saved_send,
    saved_recv,
    twin_sem,
    part_send,
    part_recv,
    peer_send,
    peer_recv,
    small_send,
    small_recv,
):
    pipes, yside = sides
    experts = yside // 2
    rounds = yside // 2
    tok_dev = ids_ref.shape[2]
    tokens = tok_dev * MICRO
    lanes = ROW * UNIT
    hid = saved.shape[1]
    fcols = weight.shape[1]
    pipe = lax.axis_index("pipe")
    place = lax.axis_index("expert")
    y = place // ROW
    zc = place % ROW
    z = zc // 2
    core = zc % 2
    z_line = z % LINE
    z_base = z - z_line
    before = lax.rem(pipe + pipes - 1, pipes)
    after = lax.rem(pipe + 1, pipes)
    expert = y // 2

    def remote(source, target, send, recv, where, section=pipe):
        return pltpu.make_async_remote_copy(
            src_ref=source,
            dst_ref=target,
            send_sem=send,
            recv_sem=recv,
            device_id=(section, where),
            device_id_type=MESH,
        )

    def source_of(y_at, turn):
        return lax.rem(jnp.where(y_at % 2 == 0, y_at + yside - turn, y_at + turn), yside)

    barrier = pltpu.get_barrier_semaphore()

    def greet(where, section=pipe):
        pl.semaphore_signal(barrier, inc=1, device_id=(section, where), device_id_type=MESH)

    greet(place, before)
    for turn in range(rounds):
        greet(source_of(y, turn) * ROW + zc, after)
    for offset in range(1, ROW):
        greet(y * ROW + lax.rem(zc + offset, ROW))
    for offset in range(1, yside):
        greet(lax.rem(y + offset, yside) * ROW + zc)

    load_rows = fetched(rows_hbm, rows, load_sem.at[0])
    load_rows.start()
    load_saved = fetched(saved_hbm, saved, load_sem.at[2])
    load_saved.start()
    load_weight = fetched(weight_hbm, weight, load_sem.at[1])
    load_weight.start()

    ids = jnp.concatenate([ids_ref[micro] for micro in range(MICRO)], axis=1)
    gates = jnp.concatenate([gates_ref[micro] for micro in range(MICRO)], axis=1)
    first = lax.broadcasted_iota(jnp.int32, (tokens, tokens), 0)
    second = lax.broadcasted_iota(jnp.int32, (tokens, tokens), 1)
    earlier = ((first < second) & (first // tok_dev == second // tok_dev)).astype(F32).astype(BF16)
    hits = []
    gate_tok = []
    for number in range(experts):
        named = ids == number
        hit = jnp.max(jnp.where(named, 1.0, 0.0), axis=0, keepdims=True)
        hits.append(jnp.broadcast_to(hit, (UNIT, tokens)))
        picked = jnp.sum(jnp.where(named, gates, 0.0), axis=0, keepdims=True)
        gate_tok.append(jnp.broadcast_to(picked, (UNIT, tokens)))
    hits = jnp.concatenate(hits, axis=0)
    gate_tok = jnp.concatenate(gate_tok, axis=0)
    rank = jnp.dot(hits.astype(BF16), earlier, preferred_element_type=F32)
    unit_row = lax.broadcasted_iota(jnp.int32, (experts * UNIT, tokens), 0) % UNIT
    token = lax.broadcasted_iota(jnp.int32, (experts * UNIT, tokens), 1)
    pick = jnp.where(
        (rank == (unit_row % CAP).astype(F32)) & (token // tok_dev == unit_row // CAP), hits, 0.0
    )
    pick_out[...] = pick.astype(BF16)
    pl.semaphore_wait(barrier, 1 + rounds + ROW - 1 + yside - 1)
    send_pick = remote(pick_out, pick_in, pick_sem.at[0], pick_sem.at[1], place, after)
    send_pick.start()

    def row_cast(source, target, kind):
        own = fetched(source, target.at[zc], small_recv.at[kind])
        own.start()

        @pl.loop(1, ROW)
        def _(offset):
            peer = lax.rem(zc + offset, ROW)
            remote(
                source, target.at[zc], small_send.at[kind], small_recv.at[kind], y * ROW + peer
            ).start()

    def column_cast(source, target, kind):
        own = fetched(source, target.at[y], small_recv.at[kind])
        own.start()

        @pl.loop(1, yside)
        def _(offset):
            peer = lax.rem(y + offset, yside)
            remote(
                source, target.at[y], small_send.at[kind], small_recv.at[kind], peer * ROW + zc
            ).start()

    slot_row = lax.broadcasted_iota(jnp.int32, (experts * UNIT, lanes), 0) % UNIT
    slot_lane = lax.broadcasted_iota(jnp.int32, (experts * UNIT, lanes), 1)
    mine = slot_lane == zc * UNIT + slot_row
    gate_slot = jnp.sum(pick * gate_tok, axis=1, keepdims=True).astype(BF16).astype(F32)
    gate_lane = jnp.where(mine, gate_slot, 0.0)
    pieces = [
        jnp.sum(gate_lane[number * UNIT : (number + 1) * UNIT], axis=0, keepdims=True)
        for number in range(experts)
    ]
    pieces += [jnp.zeros((8 - experts, lanes), F32)]
    gate_src[...] = jnp.concatenate(pieces, axis=0)
    row_cast(gate_src, gate_row, 0)

    line_row = lax.broadcasted_iota(jnp.int32, (lanes, lanes), 0)
    line_col = lax.broadcasted_iota(jnp.int32, (lanes, lanes), 1)
    per_micro = ROW * CAP
    micro_of = line_row // per_micro
    within = line_row % per_micro
    order = (line_col == (within // CAP) * UNIT + micro_of * CAP + within % CAP).astype(F32).astype(BF16)
    load_saved.wait()
    for number in range(yside):
        block = jnp.concatenate(
            [
                saved[micro, :, number * per_micro : (number + 1) * per_micro]
                for micro in range(MICRO)
            ],
            axis=1,
        )
        saved_all[core, z_line, number] = jnp.dot(
            block, order, preferred_element_type=F32
        ).astype(BF16)
    for offset in range(1, LINE):
        target = z_base + lax.rem(z_line + offset, LINE)
        remote(
            saved_all.at[core, z_line],
            saved_all.at[core, z_line],
            saved_send.at[offset],
            saved_recv.at[offset],
            y * ROW + target * 2 + core,
        ).start()

    load_rows.wait()
    send_pick.wait_recv()
    chosen = pick_in[...]
    for block in range(2 * LINE):
        taken = jnp.dot(
            chosen, rows[:, block * fcols : (block + 1) * fcols], preferred_element_type=F32
        )
        for number in range(experts):
            row_out[number, block] = taken[number * UNIT : (number + 1) * UNIT].astype(BF16)
    hops = []
    for turn in range(rounds):
        even = (y + turn) % 2 == 0
        y_to = lax.rem(jnp.where(even, y + turn, y + yside - turn), yside)
        hop = remote(
            row_out.at[y_to // 2],
            row_in.at[turn],
            hop_send.at[turn],
            hop_recv.at[turn],
            y_to * ROW + zc,
            before,
        )
        hops.append(hop)
    hops[0].start()

    way = 1 - 2 * core
    deltas = [sign * step for step in range(1, LINE) for sign in (1, -1)] + [LINE, 0]

    def spread(turn):
        hops[turn].wait()
        if turn + 1 < rounds:
            hops[turn + 1].start()
        slot = source_of(y, turn) * ROW + zc
        own = fetched(
            row_in.at[turn, z_line * 2 + core], disp.at[slot], row_recv.at[turn]
        )
        own.start()
        for delta in deltas:
            z_to = lax.rem(z + ZSIDE + delta * way, ZSIDE)
            for side in range(2):
                if delta == 0 and side == 0:
                    continue
                c_to = lax.rem(core + side, 2)
                remote(
                    row_in.at[turn, lax.rem(z_to, LINE) * 2 + c_to],
                    disp.at[slot],
                    row_send.at[turn],
                    row_recv.at[turn],
                    y * ROW + z_to * 2 + c_to,
                ).start()

    partner = jnp.where(y % 2 == 0, y + 1, y - 1)
    parity = z_line % 2
    upper = z_line // 2

    def folds(step):
        return LINE == 4 and step < yside - DIRECT

    twin = y * ROW + z * 2 + (1 - core)
    shares = []

    def receive(step, owned, turn):
        if owned:
            source = source_of(y, turn)
            region = disp.at[pl.ds(source * ROW, ROW)]
            arrived(region, row_recv.at[turn])
            remote(
                region, region, side_send.at[turn], side_recv.at[turn], partner * ROW + zc
            ).start()
        else:
            source = source_of(partner, turn)
            region = disp.at[pl.ds(source * ROW, ROW)]
            arrived(region, side_recv.at[turn])
        value = disp[pl.ds(source * ROW, ROW)].reshape(ROW * UNIT, fcols)
        product = lax.dot_general(
            weight[...], value, (((1,), (1,)), ((), ())), preferred_element_type=F32
        )
        part[step] = product.reshape(LINE, 2, hid, lanes)
        share = remote(
            part.at[step, :, 1 - core],
            part_in.at[step],
            part_send.at[step],
            part_recv.at[step],
            twin,
        )
        share.start()
        shares.append((source, share))
        if step == 0:
            arrived(saved_all.at[1 - core], twin_sem.at[1])
        score = jnp.zeros((hid, lanes), F32)
        for line in range(LINE):
            for side in range(2):
                at = (line * 2 + side) * hid
                score += saved_all[side, line, source].astype(F32) * product[at : at + hid]
        score_src[step] = jnp.sum(score, axis=0, keepdims=True)
        if owned and turn == 0:
            fetched(score_src.at[step], score_col.at[y], small_recv.at[2]).start()
        else:
            remote(
                score_src.at[step],
                score_col.at[y],
                small_send.at[2],
                small_recv.at[2],
                source * ROW + zc,
            ).start()

    def pass_on(step):
        shares[step][1].wait_recv()
        peer_out[step] = (part[step, :, core] + part_in[step]).astype(BF16)
        if folds(step):
            near = z_base + z_line + 1 - 2 * parity
            for pair in range(2):
                remote(
                    peer_out.at[step, 1 - parity + 2 * pair],
                    peer_in.at[step, 1 + pair],
                    peer_send.at[step, 1 + pair],
                    peer_recv.at[step, 1 + pair],
                    y * ROW + near * 2 + core,
                ).start()
            return
        for offset in range(1, LINE):
            target = lax.rem(z_line + offset, LINE)
            remote(
                peer_out.at[step, target],
                peer_in.at[step, offset],
                peer_send.at[step, offset],
                peer_recv.at[step, offset],
                y * ROW + (z_base + target) * 2 + core,
            ).start()

    def fold(step):
        for pair in range(2):
            arrived(peer_in.at[step, 1 + pair], peer_recv.at[step, 1 + pair])
        away = parity + 2 * (1 - upper)
        fold_out[step] = (
            part[step, away, core]
            + part_in[step, away]
            + peer_in[step, 2 - upper].astype(F32)
        ).astype(BF16)
        remote(
            fold_out.at[step],
            peer_in.at[step, 3],
            peer_send.at[step, 3],
            peer_recv.at[step, 3],
            y * ROW + (z_base + away) * 2 + core,
        ).start()

    def finish(step):
        source = shares[step][0]
        if folds(step):
            arrived(peer_in.at[step, 3], peer_recv.at[step, 3])
        else:
            for offset in range(1, LINE):
                arrived(peer_in.at[step, offset], peer_recv.at[step, offset])
        whole = part[step, z_line, core] + part_in[step, z_line]
        if folds(step):
            whole = whole + peer_in[step, 1 + upper].astype(F32) + peer_in[step, 3].astype(F32)
        else:
            for offset in range(1, LINE):
                whole = whole + peer_in[step, offset].astype(F32)
        gated = (gate_all[source, pl.ds(expert, 1), :] * whole).astype(BF16)
        turned_all[source] = lax.dot_general(
            gated, order, (((1,), (1,)), ((), ())), preferred_element_type=F32
        ).astype(BF16)

    def grow(step):
        source = shares[step][0]
        scale = gate_all[source, pl.ds(expert, 1), :]
        left = jnp.concatenate(
            [
                (saved_all[side, line, source].astype(F32) * scale).astype(BF16)
                for line in range(LINE)
                for side in range(2)
            ],
            axis=0,
        )
        value = disp[pl.ds(source * ROW, ROW)].reshape(ROW * UNIT, fcols)
        update = jnp.dot(left, value, preferred_element_type=F32)
        if step > 0:
            update = total[...] + update
        if step < yside - 1:
            total[...] = update
        else:
            down_out[...] = update.astype(BF16)

    plan = []
    for turn in range(rounds):
        plan.append((True, turn))
        if turn >= 1:
            plan.append((False, turn - 1))
    plan.append((False, rounds - 1))

    spread(0)
    arrived(gate_row, small_recv.at[0])
    summed = gate_row[0]
    for number in range(1, ROW):
        summed = summed + gate_row[number]
    gate_mid[...] = summed
    column_cast(gate_mid, gate_all, 1)
    for turn in range(1, min(DEPTH, rounds)):
        spread(turn)
    for offset in range(1, LINE):
        origin = lax.rem(z_line + LINE - offset, LINE)
        arrived(saved_all.at[core, origin], saved_recv.at[offset])
    share_saved = remote(
        saved_all.at[core], saved_all.at[core], twin_sem.at[0], twin_sem.at[1], twin
    )
    share_saved.start()
    load_weight.wait()
    for step, (owned, turn) in enumerate(plan):
        if owned and turn + DEPTH < rounds:
            arrived(disp.at[pl.ds(0, ROW - 1)], row_send.at[turn])
            spread(turn + DEPTH)
        receive(step, owned, turn)
        if step == 0:
            arrived(gate_all, small_recv.at[1])
        if step >= 1:
            pass_on(step - 1)
        grow(step)
        if step >= 2 and folds(step - 2):
            fold(step - 2)
        if step >= 3:
            finish(step - 3)
    last = len(plan) - 1
    pass_on(last)
    arrived(score_col, small_recv.at[2])
    lines = [score_col[2 * number] + score_col[2 * number + 1] for number in range(experts)]
    lines += [jnp.zeros((8 - experts, lanes), F32)]
    score_mid[...] = jnp.concatenate(lines, axis=0)
    row_cast(score_mid, score_row, 3)
    for step in range(max(last - 1, 0), last + 1):
        if folds(step):
            fold(step)
    for step in range(max(last - 2, 0), last):
        finish(step)
    finish(last)
    for micro in range(MICRO):
        hidden_out[micro] = jnp.concatenate(
            [
                turned_all[number, :, micro * per_micro : (micro + 1) * per_micro]
                for number in range(yside)
            ],
            axis=1,
        )
    arrived(score_row, small_recv.at[3])
    summed = score_row[0]
    for number in range(1, ROW):
        summed = summed + score_row[number]
    lines = [
        jnp.broadcast_to(summed[number : number + 1], (UNIT, lanes)) for number in range(experts)
    ]
    slot_score = jnp.sum(
        jnp.where(mine, jnp.concatenate(lines, axis=0), 0.0), axis=1, keepdims=True
    )
    spread_score = pick * slot_score
    result = jnp.zeros(ids.shape, F32)
    for number in range(experts):
        by_token = jnp.sum(
            spread_score[number * UNIT : (number + 1) * UNIT], axis=0, keepdims=True
        )
        result = result + jnp.where(ids == number, by_token, 0.0)
    for micro in range(MICRO):
        gate_out[micro] = result[:, micro * tok_dev : (micro + 1) * tok_dev]

    send_pick.wait_send()
    for turn in range(rounds):
        if turn + DEPTH >= rounds:
            arrived(disp.at[pl.ds(0, ROW - 1)], row_send.at[turn])
        arrived(disp.at[pl.ds(0, ROW)], side_send.at[turn])
    for offset in range(1, LINE):
        arrived(saved_all.at[0, 0], saved_send.at[offset])
    share_saved.wait_send()
    for step in range(len(plan)):
        shares[step][1].wait_send()
        for offset in range(1, LINE):
            arrived(peer_out.at[step, 0], peer_send.at[step, offset])
    for kind, count, block in (
        (0, ROW - 1, gate_row),
        (1, yside - 1, gate_all),
        (2, yside - 1, score_col),
        (3, ROW - 1, score_row),
    ):
        arrived(block.at[pl.ds(0, count)], small_send.at[kind])


def publish(hidden_ref, down_ref, gate_ref, hidden_to, down_to, gate_to):
    hidden_to[...] = hidden_ref[...]
    down_to[...] = down_ref[...]
    gate_to[...] = gate_ref[...]


def body(out_grad, expert_ids, gate_values, down_tiles, hidden_saved):
    pipes = lax.axis_size("pipe")
    devices = lax.axis_size("expert")
    yside = devices // ROW
    rounds = yside // 2
    steps = yside
    experts = yside // 2
    _, micro, tok_dev, width = out_grad.shape
    _, _, tile_rows, tile_cols = down_tiles.shape
    _, _, slots, hid = hidden_saved.shape
    topk = expert_ids.shape[-1]
    tokens = micro * tok_dev
    lanes = ROW * UNIT
    ids = expert_ids.transpose(0, 1, 3, 2).reshape(micro, topk, tok_dev)
    gates = gate_values.transpose(0, 1, 3, 2).reshape(micro, topk, tok_dev)
    saved = hidden_saved.transpose(0, 1, 3, 2).reshape(micro, hid, slots)
    vmem = pl.BlockSpec(memory_space=pltpu.VMEM)
    far = pl.BlockSpec(memory_space=pltpu.HBM)
    dma = pltpu.SemaphoreType.DMA
    hidden_grad, down_grad, gate_grad = pl.pallas_call(
        lambda *refs: relay_kernel((pipes, yside), *refs),
        out_shape=(
            jax.ShapeDtypeStruct((micro, hid, slots), BF16),
            jax.ShapeDtypeStruct((tile_rows, tile_cols), BF16),
            jax.ShapeDtypeStruct((micro, topk, tok_dev), F32),
        ),
        in_specs=[vmem, vmem, far, far, far],
        out_specs=(vmem, vmem, vmem),
        scratch_shapes=[
            pltpu.VMEM((tokens, width), BF16),
            pltpu.VMEM((tile_rows, tile_cols), BF16),
            pltpu.VMEM((micro, hid, slots), BF16),
            pltpu.VMEM((experts * UNIT, tokens), BF16),
            pltpu.VMEM((experts * UNIT, tokens), BF16),
            pltpu.VMEM((experts, 2 * LINE, UNIT, tile_cols), BF16),
            pltpu.VMEM((rounds, 2 * LINE, UNIT, tile_cols), BF16),
            pltpu.VMEM((devices, UNIT, tile_cols), BF16),
            pltpu.VMEM((2, LINE, yside, hid, lanes), BF16),
            pltpu.VMEM((tile_rows, tile_cols), F32),
            pltpu.VMEM((steps, LINE, 2, hid, lanes), F32),
            pltpu.VMEM((steps, LINE, hid, lanes), F32),
            pltpu.VMEM((steps, LINE, hid, lanes), BF16),
            pltpu.VMEM((steps, LINE, hid, lanes), BF16),
            pltpu.VMEM((steps, hid, lanes), BF16),
            pltpu.VMEM((8, lanes), F32),
            pltpu.VMEM((ROW, 8, lanes), F32),
            pltpu.VMEM((8, lanes), F32),
            pltpu.VMEM((yside, 8, lanes), F32),
            pltpu.VMEM((yside, 1, lanes), F32),
            pltpu.VMEM((yside, 1, lanes), F32),
            pltpu.VMEM((8, lanes), F32),
            pltpu.VMEM((ROW, 8, lanes), F32),
            pltpu.VMEM((yside, hid, lanes), BF16),
            dma((3,)),
            dma((2,)),
            *[dma((rounds,)) for _ in range(6)],
            dma((LINE,)),
            dma((LINE,)),
            dma((2,)),
            dma((steps,)),
            dma((steps,)),
            dma((steps, LINE)),
            dma((steps, LINE)),
            dma((4,)),
            dma((4,)),
        ],
        compiler_params=pltpu.CompilerParams(
            has_side_effects=True, collective_id=0, vmem_limit_bytes=62 * 2**20
        ),
        name="relay",
    )(
        ids,
        gates,
        out_grad.reshape(tokens, width),
        down_tiles.reshape(tile_rows, tile_cols),
        saved,
    )
    hidden_grad, down_grad, gate_grad = pl.pallas_call(
        publish,
        out_shape=tuple(
            jax.ShapeDtypeStruct(value.shape, value.dtype)
            for value in (hidden_grad, down_grad, gate_grad)
        ),
        in_specs=[vmem, vmem, vmem],
        out_specs=(vmem, vmem, vmem),
        compiler_params=pltpu.CompilerParams(vmem_limit_bytes=62 * 2**20),
        name="publish",
    )(hidden_grad, down_grad, gate_grad)
    return (
        hidden_grad.reshape(1, micro, hid, slots).transpose(0, 1, 3, 2),
        down_grad.reshape(1, 1, tile_rows, tile_cols),
        gate_grad.reshape(1, micro, topk, tok_dev).transpose(0, 1, 3, 2),
    )


def solution(mesh):
    return jax.shard_map(
        body,
        mesh=mesh,
        in_specs=(
            P("pipe", None, "expert", None),
            P("pipe", None, "expert", None),
            P("pipe", None, "expert", None),
            P("pipe", "expert", None, None),
            P("pipe", None, None, "expert"),
        ),
        out_specs=(
            P("pipe", None, None, "expert"),
            P("pipe", "expert", None, None),
            P("pipe", None, "expert", None),
        ),
        check_vma=False,
    )
```

```python
import jax
import jax.numpy as jnp
from jax import lax
from jax.experimental import pallas as pl
from jax.experimental.pallas import tpu as pltpu
from jax.sharding import PartitionSpec as P

MICRO = 2
CAP = 4
UNIT = MICRO * CAP
ZSIDE = 8
ROW = 2 * ZSIDE
LINE = ZSIDE // 2
DEPTH = 2
DIRECT = 2
MESH = pl.DeviceIdType.MESH
F32 = jnp.float32
BF16 = jnp.bfloat16


def fetched(source, target, sem):
    return pltpu.make_async_copy(source, target, sem)


def arrived(block, sem):
    pltpu.make_async_copy(block, block, sem).wait()


def relay_kernel(
    sides,
    ids_ref,
    gates_ref,
    rows_hbm,
    weight_hbm,
    saved_hbm,
    hidden_out,
    down_out,
    gate_out,
    rows,
    weight,
    saved,
    pick_out,
    pick_in,
    row_out,
    row_in,
    disp,
    saved_all,
    total,
    down_held,
    part,
    part_in,
    peer_out,
    peer_in,
    fold_out,
    gate_src,
    gate_row,
    gate_mid,
    gate_all,
    score_src,
    score_col,
    score_mid,
    score_row,
    turned_all,
    load_sem,
    pick_sem,
    hop_send,
    hop_recv,
    row_send,
    row_recv,
    side_send,
    side_recv,
    saved_send,
    saved_recv,
    twin_sem,
    part_send,
    part_recv,
    peer_send,
    peer_recv,
    small_send,
    small_recv,
):
    pipes, yside = sides
    experts = yside // 2
    rounds = yside // 2
    tok_dev = ids_ref.shape[2]
    tokens = tok_dev * MICRO
    lanes = ROW * UNIT
    hid = saved.shape[1]
    fcols = weight.shape[1]
    pipe = lax.axis_index("pipe")
    place = lax.axis_index("expert")
    y = place // ROW
    zc = place % ROW
    z = zc // 2
    core = zc % 2
    z_line = z % LINE
    z_base = z - z_line
    before = lax.rem(pipe + pipes - 1, pipes)
    after = lax.rem(pipe + 1, pipes)
    expert = y // 2

    def remote(source, target, send, recv, where, section=pipe):
        return pltpu.make_async_remote_copy(
            src_ref=source,
            dst_ref=target,
            send_sem=send,
            recv_sem=recv,
            device_id=(section, where),
            device_id_type=MESH,
        )

    def source_of(y_at, turn):
        return lax.rem(jnp.where(y_at % 2 == 0, y_at + yside - turn, y_at + turn), yside)

    barrier = pltpu.get_barrier_semaphore()

    def greet(where, section=pipe):
        pl.semaphore_signal(barrier, inc=1, device_id=(section, where), device_id_type=MESH)

    greet(place, before)
    for turn in range(rounds):
        greet(source_of(y, turn) * ROW + zc, after)
    for offset in range(1, ROW):
        greet(y * ROW + lax.rem(zc + offset, ROW))
    for offset in range(1, yside):
        greet(lax.rem(y + offset, yside) * ROW + zc)

    load_rows = fetched(rows_hbm, rows, load_sem.at[0])
    load_rows.start()
    load_saved = fetched(saved_hbm, saved, load_sem.at[2])
    load_saved.start()
    load_weight = fetched(weight_hbm, weight, load_sem.at[1])
    load_weight.start()

    ids = jnp.concatenate([ids_ref[micro] for micro in range(MICRO)], axis=1)
    gates = jnp.concatenate([gates_ref[micro] for micro in range(MICRO)], axis=1)
    first = lax.broadcasted_iota(jnp.int32, (tokens, tokens), 0)
    second = lax.broadcasted_iota(jnp.int32, (tokens, tokens), 1)
    earlier = ((first < second) & (first // tok_dev == second // tok_dev)).astype(F32).astype(BF16)
    hits = []
    gate_tok = []
    for number in range(experts):
        named = ids == number
        hit = jnp.max(jnp.where(named, 1.0, 0.0), axis=0, keepdims=True)
        hits.append(jnp.broadcast_to(hit, (UNIT, tokens)))
        picked = jnp.sum(jnp.where(named, gates, 0.0), axis=0, keepdims=True)
        gate_tok.append(jnp.broadcast_to(picked, (UNIT, tokens)))
    hits = jnp.concatenate(hits, axis=0)
    gate_tok = jnp.concatenate(gate_tok, axis=0)
    rank = jnp.dot(hits.astype(BF16), earlier, preferred_element_type=F32)
    unit_row = lax.broadcasted_iota(jnp.int32, (experts * UNIT, tokens), 0) % UNIT
    token = lax.broadcasted_iota(jnp.int32, (experts * UNIT, tokens), 1)
    pick = jnp.where(
        (rank == (unit_row % CAP).astype(F32)) & (token // tok_dev == unit_row // CAP), hits, 0.0
    )
    pick_out[...] = pick.astype(BF16)
    pl.semaphore_wait(barrier, 1 + rounds + ROW - 1 + yside - 1)
    send_pick = remote(pick_out, pick_in, pick_sem.at[0], pick_sem.at[1], place, after)
    send_pick.start()

    def row_cast(source, target, kind):
        own = fetched(source, target.at[zc], small_recv.at[kind])
        own.start()

        @pl.loop(1, ROW)
        def _(offset):
            peer = lax.rem(zc + offset, ROW)
            remote(
                source, target.at[zc], small_send.at[kind], small_recv.at[kind], y * ROW + peer
            ).start()

    def column_cast(source, target, kind):
        own = fetched(source, target.at[y], small_recv.at[kind])
        own.start()

        @pl.loop(1, yside)
        def _(offset):
            peer = lax.rem(y + offset, yside)
            remote(
                source, target.at[y], small_send.at[kind], small_recv.at[kind], peer * ROW + zc
            ).start()

    slot_row = lax.broadcasted_iota(jnp.int32, (experts * UNIT, lanes), 0) % UNIT
    slot_lane = lax.broadcasted_iota(jnp.int32, (experts * UNIT, lanes), 1)
    mine = slot_lane == zc * UNIT + slot_row
    gate_slot = jnp.sum(pick * gate_tok, axis=1, keepdims=True).astype(BF16).astype(F32)
    gate_lane = jnp.where(mine, gate_slot, 0.0)
    pieces = [
        jnp.sum(gate_lane[number * UNIT : (number + 1) * UNIT], axis=0, keepdims=True)
        for number in range(experts)
    ]
    pieces += [jnp.zeros((8 - experts, lanes), F32)]
    gate_src[...] = jnp.concatenate(pieces, axis=0)
    row_cast(gate_src, gate_row, 0)

    line_row = lax.broadcasted_iota(jnp.int32, (lanes, lanes), 0)
    line_col = lax.broadcasted_iota(jnp.int32, (lanes, lanes), 1)
    per_micro = ROW * CAP
    micro_of = line_row // per_micro
    within = line_row % per_micro
    order = (line_col == (within // CAP) * UNIT + micro_of * CAP + within % CAP).astype(F32).astype(BF16)
    load_saved.wait()
    for number in range(yside):
        block = jnp.concatenate(
            [
                saved[micro, :, number * per_micro : (number + 1) * per_micro]
                for micro in range(MICRO)
            ],
            axis=1,
        )
        saved_all[core, z_line, number] = jnp.dot(
            block, order, preferred_element_type=F32
        ).astype(BF16)
    for offset in range(1, LINE):
        target = z_base + lax.rem(z_line + offset, LINE)
        remote(
            saved_all.at[core, z_line],
            saved_all.at[core, z_line],
            saved_send.at[offset],
            saved_recv.at[offset],
            y * ROW + target * 2 + core,
        ).start()

    load_rows.wait()
    send_pick.wait_recv()
    chosen = pick_in[...]
    for block in range(2 * LINE):
        taken = jnp.dot(
            chosen, rows[:, block * fcols : (block + 1) * fcols], preferred_element_type=F32
        )
        for number in range(experts):
            row_out[number, block] = taken[number * UNIT : (number + 1) * UNIT].astype(BF16)
    hops = []
    for turn in range(rounds):
        even = (y + turn) % 2 == 0
        y_to = lax.rem(jnp.where(even, y + turn, y + yside - turn), yside)
        hop = remote(
            row_out.at[y_to // 2],
            row_in.at[turn],
            hop_send.at[turn],
            hop_recv.at[turn],
            y_to * ROW + zc,
            before,
        )
        hops.append(hop)
    hops[0].start()

    way = 1 - 2 * core
    deltas = [sign * step for step in range(1, LINE) for sign in (1, -1)] + [LINE, 0]

    def spread(turn):
        hops[turn].wait()
        if turn + 1 < rounds:
            hops[turn + 1].start()
        slot = source_of(y, turn) * ROW + zc
        own = fetched(
            row_in.at[turn, z_line * 2 + core], disp.at[slot], row_recv.at[turn]
        )
        own.start()
        for delta in deltas:
            z_to = lax.rem(z + ZSIDE + delta * way, ZSIDE)
            for side in range(2):
                if delta == 0 and side == 0:
                    continue
                c_to = lax.rem(core + side, 2)
                remote(
                    row_in.at[turn, lax.rem(z_to, LINE) * 2 + c_to],
                    disp.at[slot],
                    row_send.at[turn],
                    row_recv.at[turn],
                    y * ROW + z_to * 2 + c_to,
                ).start()

    partner = jnp.where(y % 2 == 0, y + 1, y - 1)
    parity = z_line % 2
    upper = z_line // 2

    def folds(step):
        return LINE == 4 and step < yside - DIRECT

    twin = y * ROW + z * 2 + (1 - core)
    shares = []

    def receive(step, owned, turn):
        if owned:
            source = source_of(y, turn)
            region = disp.at[pl.ds(source * ROW, ROW)]
            arrived(region, row_recv.at[turn])
            remote(
                region, region, side_send.at[turn], side_recv.at[turn], partner * ROW + zc
            ).start()
        else:
            source = source_of(partner, turn)
            region = disp.at[pl.ds(source * ROW, ROW)]
            arrived(region, side_recv.at[turn])
        value = disp[pl.ds(source * ROW, ROW)].reshape(ROW * UNIT, fcols)
        product = lax.dot_general(
            weight[...], value, (((1,), (1,)), ((), ())), preferred_element_type=F32
        )
        part[step] = product.reshape(LINE, 2, hid, lanes)
        share = remote(
            part.at[step, :, 1 - core],
            part_in.at[step],
            part_send.at[step],
            part_recv.at[step],
            twin,
        )
        share.start()
        shares.append((source, share))
        if step == 0:
            arrived(saved_all.at[1 - core], twin_sem.at[1])
        score = jnp.zeros((hid, lanes), F32)
        for line in range(LINE):
            for side in range(2):
                at = (line * 2 + side) * hid
                score += saved_all[side, line, source].astype(F32) * product[at : at + hid]
        score_src[step] = jnp.sum(score, axis=0, keepdims=True)
        if owned and turn == 0:
            fetched(score_src.at[step], score_col.at[y], small_recv.at[2]).start()
        else:
            remote(
                score_src.at[step],
                score_col.at[y],
                small_send.at[2],
                small_recv.at[2],
                source * ROW + zc,
            ).start()

    def pass_on(step):
        shares[step][1].wait_recv()
        peer_out[step] = (part[step, :, core] + part_in[step]).astype(BF16)
        if folds(step):
            near = z_base + z_line + 1 - 2 * parity
            for pair in range(2):
                remote(
                    peer_out.at[step, 1 - parity + 2 * pair],
                    peer_in.at[step, 1 + pair],
                    peer_send.at[step, 1 + pair],
                    peer_recv.at[step, 1 + pair],
                    y * ROW + near * 2 + core,
                ).start()
            return
        for offset in range(1, LINE):
            target = lax.rem(z_line + offset, LINE)
            remote(
                peer_out.at[step, target],
                peer_in.at[step, offset],
                peer_send.at[step, offset],
                peer_recv.at[step, offset],
                y * ROW + (z_base + target) * 2 + core,
            ).start()

    def fold(step):
        for pair in range(2):
            arrived(peer_in.at[step, 1 + pair], peer_recv.at[step, 1 + pair])
        away = parity + 2 * (1 - upper)
        fold_out[step] = (
            part[step, away, core]
            + part_in[step, away]
            + peer_in[step, 2 - upper].astype(F32)
        ).astype(BF16)
        remote(
            fold_out.at[step],
            peer_in.at[step, 3],
            peer_send.at[step, 3],
            peer_recv.at[step, 3],
            y * ROW + (z_base + away) * 2 + core,
        ).start()

    def finish(step):
        source = shares[step][0]
        if folds(step):
            arrived(peer_in.at[step, 3], peer_recv.at[step, 3])
        else:
            for offset in range(1, LINE):
                arrived(peer_in.at[step, offset], peer_recv.at[step, offset])
        whole = part[step, z_line, core] + part_in[step, z_line]
        if folds(step):
            whole = whole + peer_in[step, 1 + upper].astype(F32) + peer_in[step, 3].astype(F32)
        else:
            for offset in range(1, LINE):
                whole = whole + peer_in[step, offset].astype(F32)
        gated = (gate_all[source, pl.ds(expert, 1), :] * whole).astype(BF16)
        turned_all[source] = lax.dot_general(
            gated, order, (((1,), (1,)), ((), ())), preferred_element_type=F32
        ).astype(BF16)

    def grow(step):
        source = shares[step][0]
        scale = gate_all[source, pl.ds(expert, 1), :]
        left = jnp.concatenate(
            [
                (saved_all[side, line, source].astype(F32) * scale).astype(BF16)
                for line in range(LINE)
                for side in range(2)
            ],
            axis=0,
        )
        value = disp[pl.ds(source * ROW, ROW)].reshape(ROW * UNIT, fcols)
        update = jnp.dot(left, value, preferred_element_type=F32)
        if step > 0:
            update = total[...] + update
        if step < yside - 1:
            total[...] = update
        else:
            down_held[...] = update.astype(BF16)
            fetched(down_held, down_out, load_sem.at[3]).start()

    plan = []
    for turn in range(rounds):
        plan.append((True, turn))
        if turn >= 1:
            plan.append((False, turn - 1))
    plan.append((False, rounds - 1))

    spread(0)
    arrived(gate_row, small_recv.at[0])
    summed = gate_row[0]
    for number in range(1, ROW):
        summed = summed + gate_row[number]
    gate_mid[...] = summed
    column_cast(gate_mid, gate_all, 1)
    for turn in range(1, min(DEPTH, rounds)):
        spread(turn)
    for offset in range(1, LINE):
        origin = lax.rem(z_line + LINE - offset, LINE)
        arrived(saved_all.at[core, origin], saved_recv.at[offset])
    share_saved = remote(
        saved_all.at[core], saved_all.at[core], twin_sem.at[0], twin_sem.at[1], twin
    )
    share_saved.start()
    load_weight.wait()
    for step, (owned, turn) in enumerate(plan):
        if owned and turn + DEPTH < rounds:
            arrived(disp.at[pl.ds(0, ROW - 1)], row_send.at[turn])
            spread(turn + DEPTH)
        receive(step, owned, turn)
        if step == 0:
            arrived(gate_all, small_recv.at[1])
        if step >= 1:
            pass_on(step - 1)
        grow(step)
        if step >= 2 and folds(step - 2):
            fold(step - 2)
        if step >= 3:
            finish(step - 3)
    last = len(plan) - 1
    pass_on(last)
    arrived(score_col, small_recv.at[2])
    lines = [score_col[2 * number] + score_col[2 * number + 1] for number in range(experts)]
    lines += [jnp.zeros((8 - experts, lanes), F32)]
    score_mid[...] = jnp.concatenate(lines, axis=0)
    row_cast(score_mid, score_row, 3)
    for step in range(max(last - 1, 0), last + 1):
        if folds(step):
            fold(step)
    for step in range(max(last - 2, 0), last):
        finish(step)
    finish(last)
    for micro in range(MICRO):
        hidden_out[micro] = jnp.concatenate(
            [
                turned_all[number, :, micro * per_micro : (micro + 1) * per_micro]
                for number in range(yside)
            ],
            axis=1,
        )
    arrived(score_row, small_recv.at[3])
    summed = score_row[0]
    for number in range(1, ROW):
        summed = summed + score_row[number]
    lines = [
        jnp.broadcast_to(summed[number : number + 1], (UNIT, lanes)) for number in range(experts)
    ]
    slot_score = jnp.sum(
        jnp.where(mine, jnp.concatenate(lines, axis=0), 0.0), axis=1, keepdims=True
    )
    spread_score = pick * slot_score
    result = jnp.zeros(ids.shape, F32)
    for number in range(experts):
        by_token = jnp.sum(
            spread_score[number * UNIT : (number + 1) * UNIT], axis=0, keepdims=True
        )
        result = result + jnp.where(ids == number, by_token, 0.0)
    for micro in range(MICRO):
        gate_out[micro] = result[:, micro * tok_dev : (micro + 1) * tok_dev]

    arrived(down_held, load_sem.at[3])
    send_pick.wait_send()
    for turn in range(rounds):
        if turn + DEPTH >= rounds:
            arrived(disp.at[pl.ds(0, ROW - 1)], row_send.at[turn])
        arrived(disp.at[pl.ds(0, ROW)], side_send.at[turn])
    for offset in range(1, LINE):
        arrived(saved_all.at[0, 0], saved_send.at[offset])
    share_saved.wait_send()
    for step in range(len(plan)):
        shares[step][1].wait_send()
        for offset in range(1, LINE):
            arrived(peer_out.at[step, 0], peer_send.at[step, offset])
    for kind, count, block in (
        (0, ROW - 1, gate_row),
        (1, yside - 1, gate_all),
        (2, yside - 1, score_col),
        (3, ROW - 1, score_row),
    ):
        arrived(block.at[pl.ds(0, count)], small_send.at[kind])


def publish(hidden_ref, down_ref, gate_ref, hidden_to, down_to, gate_to, hidden, down, gate, sem_in, sem_out):
    half = down.shape[0] // 2
    moves = [
        (down_ref.at[pl.ds(0, half)], down.at[pl.ds(0, half)], down_to.at[pl.ds(0, half)]),
        (down_ref.at[pl.ds(half, half)], down.at[pl.ds(half, half)], down_to.at[pl.ds(half, half)]),
        (hidden_ref, hidden, hidden_to),
        (gate_ref, gate, gate_to),
    ]
    loads = [fetched(a, b, sem_in.at[k]) for k, (a, b, _) in enumerate(moves)]
    stores = [fetched(b, c, sem_out.at[k]) for k, (_, b, c) in enumerate(moves)]
    for copy in loads:
        copy.start()
    for load, store in zip(loads, stores):
        load.wait()
        store.start()
    for store in stores:
        store.wait()


def body(out_grad, expert_ids, gate_values, down_tiles, hidden_saved):
    pipes = lax.axis_size("pipe")
    devices = lax.axis_size("expert")
    yside = devices // ROW
    rounds = yside // 2
    steps = yside
    experts = yside // 2
    _, micro, tok_dev, width = out_grad.shape
    _, _, tile_rows, tile_cols = down_tiles.shape
    _, _, slots, hid = hidden_saved.shape
    topk = expert_ids.shape[-1]
    tokens = micro * tok_dev
    lanes = ROW * UNIT
    ids = expert_ids.transpose(0, 1, 3, 2).reshape(micro, topk, tok_dev)
    gates = gate_values.transpose(0, 1, 3, 2).reshape(micro, topk, tok_dev)
    saved = hidden_saved.transpose(0, 1, 3, 2).reshape(micro, hid, slots)
    vmem = pl.BlockSpec(memory_space=pltpu.VMEM)
    far = pl.BlockSpec(memory_space=pltpu.HBM)
    dma = pltpu.SemaphoreType.DMA
    hidden_grad, down_grad, gate_grad = pl.pallas_call(
        lambda *refs: relay_kernel((pipes, yside), *refs),
        out_shape=(
            jax.ShapeDtypeStruct((micro, hid, slots), BF16),
            jax.ShapeDtypeStruct((tile_rows, tile_cols), BF16),
            jax.ShapeDtypeStruct((micro, topk, tok_dev), F32),
        ),
        in_specs=[vmem, vmem, far, far, far],
        out_specs=(vmem, far, vmem),
        scratch_shapes=[
            pltpu.VMEM((tokens, width), BF16),
            pltpu.VMEM((tile_rows, tile_cols), BF16),
            pltpu.VMEM((micro, hid, slots), BF16),
            pltpu.VMEM((experts * UNIT, tokens), BF16),
            pltpu.VMEM((experts * UNIT, tokens), BF16),
            pltpu.VMEM((experts, 2 * LINE, UNIT, tile_cols), BF16),
            pltpu.VMEM((rounds, 2 * LINE, UNIT, tile_cols), BF16),
            pltpu.VMEM((devices, UNIT, tile_cols), BF16),
            pltpu.VMEM((2, LINE, yside, hid, lanes), BF16),
            pltpu.VMEM((tile_rows, tile_cols), F32),
            pltpu.VMEM((tile_rows, tile_cols), BF16),
            pltpu.VMEM((steps, LINE, 2, hid, lanes), F32),
            pltpu.VMEM((steps, LINE, hid, lanes), F32),
            pltpu.VMEM((steps, LINE, hid, lanes), BF16),
            pltpu.VMEM((steps, LINE, hid, lanes), BF16),
            pltpu.VMEM((steps, hid, lanes), BF16),
            pltpu.VMEM((8, lanes), F32),
            pltpu.VMEM((ROW, 8, lanes), F32),
            pltpu.VMEM((8, lanes), F32),
            pltpu.VMEM((yside, 8, lanes), F32),
            pltpu.VMEM((yside, 1, lanes), F32),
            pltpu.VMEM((yside, 1, lanes), F32),
            pltpu.VMEM((8, lanes), F32),
            pltpu.VMEM((ROW, 8, lanes), F32),
            pltpu.VMEM((yside, hid, lanes), BF16),
            dma((4,)),
            dma((2,)),
            *[dma((rounds,)) for _ in range(6)],
            dma((LINE,)),
            dma((LINE,)),
            dma((2,)),
            dma((steps,)),
            dma((steps,)),
            dma((steps, LINE)),
            dma((steps, LINE)),
            dma((4,)),
            dma((4,)),
        ],
        compiler_params=pltpu.CompilerParams(
            has_side_effects=True, collective_id=0, vmem_limit_bytes=62 * 2**20
        ),
        name="relay",
    )(
        ids,
        gates,
        out_grad.reshape(tokens, width),
        down_tiles.reshape(tile_rows, tile_cols),
        saved,
    )
    hidden_grad, down_grad, gate_grad = pl.pallas_call(
        publish,
        out_shape=tuple(
            jax.ShapeDtypeStruct(value.shape, value.dtype)
            for value in (hidden_grad, down_grad, gate_grad)
        ),
        in_specs=[far, far, far],
        out_specs=(far, far, far),
        scratch_shapes=[
            pltpu.VMEM((micro, hid, slots), BF16),
            pltpu.VMEM((tile_rows, tile_cols), BF16),
            pltpu.VMEM((micro, topk, tok_dev), F32),
            dma((4,)),
            dma((4,)),
        ],
        compiler_params=pltpu.CompilerParams(vmem_limit_bytes=62 * 2**20),
        name="publish",
    )(hidden_grad, down_grad, gate_grad)
    return (
        hidden_grad.reshape(1, micro, hid, slots).transpose(0, 1, 3, 2),
        down_grad.reshape(1, 1, tile_rows, tile_cols),
        gate_grad.reshape(1, micro, topk, tok_dev).transpose(0, 1, 3, 2),
    )


def solution(mesh):
    return jax.shard_map(
        body,
        mesh=mesh,
        in_specs=(
            P("pipe", None, "expert", None),
            P("pipe", None, "expert", None),
            P("pipe", None, "expert", None),
            P("pipe", "expert", None, None),
            P("pipe", None, None, "expert"),
        ),
        out_specs=(
            P("pipe", None, None, "expert"),
            P("pipe", "expert", None, None),
            P("pipe", None, "expert", None),
        ),
        check_vma=False,
    )
```
